128 devices in a mesh: ctx: 16 (over x, z_hi, core), fsdp: 8 (over y, z_lo).
Axes of the slice: x: 4, y: 4, z: 4 (z_hi: 2, z_lo: 2; z = z_hi * 2 + z_lo), core: 2. Of those that a mesh axis runs over, the one named last changes fastest.
Arguments:
- tokens: bfloat16 [8, 3072, 1024], P('fsdp', 'ctx'), may hold values from -6 to 6
- positions: int32 [8, 3072], P('fsdp', 'ctx'), may hold values from 0 to 3071, as said below
- cotangent: bfloat16 [8, 3072, 1024], P('fsdp', 'ctx'), may hold values from -6 to 6
- attn_gain: bfloat16 [1024], P('fsdp'), may hold values from 0.25 to 1.75
- w_query: bfloat16 [1024, 1024], P('fsdp'), may hold values from -0.1875 to 0.1875
- w_key: bfloat16 [1024, 512], P('fsdp'), may hold values from -0.1875 to 0.1875
- w_value: bfloat16 [1024, 512], P('fsdp'), may hold values from -0.1875 to 0.1875
- query_gain: bfloat16 [64], P('fsdp'), may hold values from 0.25 to 1.75
- key_gain: bfloat16 [64], P('fsdp'), may hold values from 0.25 to 1.75
- w_out: bfloat16 [1024, 1024], P('fsdp'), may hold values from -3 to 3
- ffn_gain: bfloat16 [1024], P('fsdp'), may hold values from 0.25 to 1.75
- w_gate: bfloat16 [1024, 4608], P('fsdp'), may hold values from -0.1875 to 0.1875
- w_up: bfloat16 [1024, 4608], P('fsdp'), may hold values from -0.1875 to 0.1875
- w_down: bfloat16 [4608, 1024], P('fsdp'), may hold values from -0.09375 to 0.09375
Outputs:
- result: bfloat16 [8, 3072, 1024], P('fsdp', 'ctx')
- grad_tokens: bfloat16 [8, 3072, 1024], P('fsdp', 'ctx')
- grad_attn_gain: float32 [1024], P('fsdp')
- grad_w_query: float32 [1024, 1024], P('fsdp')
- grad_w_key: float32 [1024, 512], P('fsdp')
- grad_w_value: float32 [1024, 512], P('fsdp')
- grad_query_gain: float32 [64], P('fsdp')
- grad_key_gain: float32 [64], P('fsdp')
- grad_w_out: float32 [1024, 1024], P('fsdp')
- grad_ffn_gain: float32 [1024], P('fsdp')
- grad_w_gate: float32 [1024, 4608], P('fsdp')
- grad_w_up: float32 [1024, 4608], P('fsdp')
- grad_w_down: float32 [4608, 1024], P('fsdp')
The draws below stay inside these ranges and needn't reach their ends.
Inputs may be any that keep to these rules, and one draw needn't show every extreme that they name: In each sequence the positions rise by one from token to token, except at one token between a quarter and three quarters of the way through the sequence, where they restart at 0; the token just before the restart has position 3071.
All inputs are finite; a program needn't handle non-finite values.
Results may differ from the reference program's by a relative error of at most 0.028.
Values may be sent and summed in bfloat16 or wider, within the bound.
No kernel may reach another device: no remote copies, remote signals or barrier semaphores. Data moves between devices by JAX's collectives and lax.ppermute only.
A program may use at most 192 MiB of HBM per device.

```python
import jax
import jax.numpy as jnp
from jax import lax

D = 1024
H = 16
KV = 8
HD = 64
FF = 4608
QW = 1024
KVW = 512
LEN = 3072
SEQS = 8


def draw_positions(key, part):
    cuts = jax.random.randint(jax.random.fold_in(key, 12), (SEQS, 1), LEN // 4, 3 * LEN // 4 + 1)
    indices = jnp.arange(LEN, dtype=jnp.int32)[None, :]
    offsets = LEN - cuts
    return jnp.where(indices < cuts, indices + offsets, indices - cuts).astype(jnp.int32)


def block_scale(own_key, extent, shards, smallest, high):
    loudness = 1.0
    for axis_at, shards_of in shards:
        steps = jax.random.uniform(jax.random.fold_in(jax.random.fold_in(own_key, 6), axis_at), (shards_of,), jnp.float32, smallest / len(shards), high / len(shards))
        loudness = loudness * jnp.repeat(jnp.exp(steps), extent[axis_at] // shards_of).reshape((-1,) + (1,) * (len(extent) - 1 - axis_at))
    return loudness


def gaussian(stream_key, dims, deviation, most, shards=(), kind=jnp.bfloat16):
    factor_of = block_scale(stream_key, dims, shards, -0.22, 0.18) if shards else 1.0
    drawn = jax.random.normal(stream_key, dims, jnp.float32) * deviation * factor_of
    return jnp.minimum(jnp.maximum(drawn, -most), most).astype(kind)


def setup_inputs(seed: int = 0) -> dict:
    seeds = jax.random.split(jax.random.key(seed), 15)
    tokens = gaussian(seeds[0], (SEQS, LEN, D), 1.0, 6.0, ((0, 8), (1, 16)))
    positions = draw_positions(jax.random.fold_in(seeds[14], 71), 0)
    cotangent = gaussian(seeds[2], (SEQS, LEN, D), 1.0, 6.0, ((0, 8), (1, 16)))
    attn_gain = jnp.clip(1.0 + 0.15 * jax.random.normal(seeds[3], (D,), jnp.float32), 0.25, 1.75).astype(jnp.bfloat16)
    w_query = gaussian(seeds[4], (D, QW), D ** -0.5, 0.1875, ((0, 8),))
    w_key = gaussian(seeds[5], (D, KVW), D ** -0.5, 0.1875, ((0, 8),))
    w_value = gaussian(seeds[6], (D, KVW), D ** -0.5, 0.1875, ((0, 8),))
    query_gain = jnp.clip(1.0 + 0.15 * jax.random.normal(seeds[7], (HD,), jnp.float32), 0.25, 1.75).astype(jnp.bfloat16)
    key_gain = jnp.clip(1.0 + 0.15 * jax.random.normal(seeds[8], (HD,), jnp.float32), 0.25, 1.75).astype(jnp.bfloat16)
    w_out = gaussian(seeds[9], (QW, D), (max(D // 256, 1)) ** -0.5, 3.0, ((0, 8),))
    ffn_gain = jnp.clip(1.0 + 0.15 * jax.random.normal(seeds[10], (D,), jnp.float32), 0.25, 1.75).astype(jnp.bfloat16)
    w_gate = gaussian(seeds[11], (D, FF), D ** -0.5, 0.1875, ((0, 8),))
    w_up = gaussian(seeds[12], (D, FF), D ** -0.5, 0.1875, ((0, 8),))
    w_down = gaussian(seeds[13], (FF, D), FF ** -0.5, 0.09375, ((0, 8),))
    return dict(tokens=tokens, positions=positions, cotangent=cotangent, attn_gain=attn_gain, w_query=w_query, w_key=w_key, w_value=w_value, query_gain=query_gain, key_gain=key_gain, w_out=w_out, ffn_gain=ffn_gain, w_gate=w_gate, w_up=w_up, w_down=w_down)


EPSILON = 1e-05
ROPE_BASE = 1000000.0
HIGHEST = lax.Precision.HIGHEST

@jax.custom_vjp
def low(v):
    return lax.optimization_barrier(v.astype(jnp.bfloat16)).astype(jnp.float32)

@jax.custom_vjp
def low_back(v):
    return v

def low_keep(v):
    return (low(v), None)

def low_pass(kept, grad):
    return (grad,)

def back_keep(v):
    return (v, None)

def back_low(kept, grad):
    return (low(grad),)
low.defvjp(low_keep, low_pass)
low_back.defvjp(back_keep, back_low)

def norm_scale(inputs):
    return lax.rsqrt(lax.optimization_barrier(jnp.mean(inputs * inputs, axis=-1, keepdims=True)) + EPSILON)

def rotary_tables(token_pos):
    halves = HD // 2
    frequency = ROPE_BASE ** (-(jnp.arange(halves, dtype=jnp.float32) * 2.0 / HD))
    angles = token_pos.astype(jnp.float32)[:, None] * frequency[None, :]
    return (jnp.cos(angles)[:, None, :], jnp.sin(angles)[:, None, :])

def rotate(inputs, cosines, sines):
    halves = inputs.shape[-1] // 2
    former = inputs[..., :halves]
    latter = inputs[..., halves:]
    return jnp.concatenate([former * cosines - latter * sines, latter * cosines + former * sines], axis=-1)

def attend_rows(query_rows, query_ids, start_ids, key_rows, value_rows):
    scores = jnp.einsum('bkgd,lkd->kgbl', query_rows, key_rows, precision=HIGHEST) * 0.125
    scores = low_back(scores)
    key_ids = jnp.arange(key_rows.shape[0], dtype=jnp.int32)
    allowed = (key_ids[None, :] <= query_ids[:, None]) & (key_ids[None, :] >= start_ids[:, None])
    scores = jnp.where(allowed[None, None], scores, -jnp.inf)
    row_top = lax.optimization_barrier(jnp.max(scores, axis=-1, keepdims=True))
    weights = jnp.exp(scores - row_top)
    probs = weights / lax.optimization_barrier(jnp.sum(weights, axis=-1, keepdims=True))
    return jnp.einsum('kgbl,lkd->bkgd', low(probs), value_rows, precision=HIGHEST)

def layer(x_float, token_pos, params):
    attn_gain, w_query, w_key, w_value, query_gain, key_gain, w_out, ffn_gain, w_gate, w_up, w_down = params
    length = x_float.shape[0]
    normed = low(x_float * norm_scale(x_float) * attn_gain)
    query_raw = low_back(jnp.dot(normed, w_query, precision=HIGHEST)).reshape(length, H, HD)
    key_raw = low_back(jnp.dot(normed, w_key, precision=HIGHEST)).reshape(length, KV, HD)
    value_rows = low(low_back(jnp.dot(normed, w_value, precision=HIGHEST))).reshape(length, KV, HD)
    cosines, sines = rotary_tables(token_pos)
    query_rot = low(rotate(query_raw * norm_scale(query_raw) * query_gain, cosines, sines))
    query_rot = query_rot.reshape(length, KV, H // KV, HD)
    key_rot = low(rotate(key_raw * norm_scale(key_raw) * key_gain, cosines, sines))
    token_ids = jnp.arange(length, dtype=jnp.int32)
    start_ids = token_ids - token_pos
    block_size = min(512, length)
    block_count = length // block_size
    attend_saved = jax.checkpoint(attend_rows)

    def one_block(pieces):
        return attend_saved(pieces[0], pieces[1], pieces[2], key_rot, value_rows)
    attended = lax.map(one_block, (query_rot.reshape(block_count, block_size, KV, H // KV, HD), token_ids.reshape(block_count, block_size), start_ids.reshape(block_count, block_size)))
    attended = low(low_back(attended.reshape(length, H * HD)))
    hidden = x_float + low_back(jnp.dot(attended, w_out, precision=HIGHEST))
    mlp_input = low(hidden * norm_scale(hidden) * ffn_gain)
    gate_proj = low_back(jnp.dot(mlp_input, w_gate, precision=HIGHEST))
    up_proj = low_back(jnp.dot(mlp_input, w_up, precision=HIGHEST))
    mlp_hidden = low(jax.nn.silu(gate_proj) * up_proj)
    return hidden + jnp.dot(mlp_hidden, w_down, precision=HIGHEST)

def reference(tokens, positions, cotangent, attn_gain, w_query, w_key, w_value, query_gain, key_gain, w_out, ffn_gain, w_gate, w_up, w_down):
    params = tuple((weight.astype(jnp.float32) for weight in (attn_gain, w_query, w_key, w_value, query_gain, key_gain, w_out, ffn_gain, w_gate, w_up, w_down)))

    def one_sequence(totals, inputs):
        seq_tokens, seq_pos, seq_grad = inputs
        output, pullback = jax.vjp(lambda inner_x, inner_params: layer(inner_x, seq_pos, inner_params), seq_tokens.astype(jnp.float32), params)
        grad_input, grad_params = pullback(seq_grad.astype(jnp.float32))
        totals = tuple((running + added for running, added in zip(totals, grad_params)))
        return (totals, (output.astype(jnp.bfloat16), grad_input.astype(jnp.bfloat16)))
    zeros_start = tuple((jnp.zeros_like(weight) for weight in params))
    totals, (outputs, grad_tokens) = lax.scan(one_sequence, zeros_start, (tokens, positions, cotangent))
    return (outputs, grad_tokens, totals[0], totals[1], totals[2], totals[3], totals[4], totals[5], totals[6], totals[7], totals[8], totals[9], totals[10])
```

```python
import functools

import jax
import jax.numpy as jnp
from jax import lax
from jax.experimental import pallas as pl
from jax.experimental.pallas import tpu as pltpu
from jax.sharding import PartitionSpec as P

EPSILON = 1e-05
ROPE_BASE = 1000000.0
F32 = jnp.float32
BF16 = jnp.bfloat16
LOG2E = 1.4426950408889634
SCALE = 0.125


def move_ctx(v, dx=0, dz=0, dc=0):
    pairs = [
        (a * 4 + b * 2 + c, ((a + dx) % 4) * 4 + (b ^ dz) * 2 + (c ^ dc))
        for a in range(4)
        for b in range(2)
        for c in range(2)
    ]
    return lax.ppermute(v, "ctx", pairs)


def move_fsdp(v, dy=0, dz=0):
    pairs = [
        (a * 2 + b, ((a + dy) % 4) * 2 + (b ^ dz)) for a in range(4) for b in range(2)
    ]
    return lax.ppermute(v, "fsdp", pairs)


def swap_roles(v):
    pairs = []
    for t in range(8):
        for h in range(2):
            for f in range(8):
                src = ((t // 2) * 4 + h * 2 + t % 2) * 8 + f
                dst = ((f // 2) * 4 + h * 2 + f % 2) * 8 + t
                pairs.append((src, dst))
    return lax.ppermute(v, ("ctx", "fsdp"), pairs)


def gather_group(u):
    one, two, three = move_ctx(u, dx=1), move_ctx(u, dx=2), move_ctx(u, dx=3)
    return [[v, move_ctx(v, dc=1)] for v in (u, one, two, three)]


def joined(blocks):
    return jnp.concatenate([b for pair in blocks for b in pair], axis=0)


def scatter_group(part):
    other = move_ctx(part[1:, 1].astype(BF16), dc=1)
    other_home = move_ctx(part[0, 1].astype(BF16), dc=1)
    total = part[0, 0].astype(F32) + other_home.astype(F32)
    for r in (1, 2, 3):
        acc = part[r, 0].astype(F32) + other[r - 1].astype(F32)
        total = total + move_ctx(acc.astype(BF16), dx=-r).astype(F32)
    return total


def exchange_group(blocks):
    other = move_ctx(jnp.stack([blocks[r][1] for r in range(4)]), dc=1)
    out = [[blocks[0][0], other[0]]]
    for r in (1, 2, 3):
        both = move_ctx(jnp.stack([blocks[r][0], other[r]]), dx=-r)
        out.append([both[0], both[1]])
    return out


def gather_fsdp(u, y, zl):
    o = move_fsdp(u, dz=1)
    low = zl == 0
    pair = jnp.stack([jnp.where(low, u, o), jnp.where(low, o, u)])
    full = jnp.zeros((4,) + pair.shape, u.dtype)
    for d in range(4):
        got = pair if d == 0 else move_fsdp(pair, dy=d)
        full = lax.dynamic_update_index_in_dim(full, got, (y - d) % 4, 0)
    return full.reshape((8,) + u.shape)


def scatter_fsdp(part, y, zl):
    part = part.reshape((4, 2) + part.shape[1:])
    give = lax.dynamic_index_in_dim(part, 1 - zl, 1, keepdims=False).astype(BF16)
    keep = lax.dynamic_index_in_dim(part, zl, 1, keepdims=False)
    acc = keep.astype(F32) + move_fsdp(give, dz=1).astype(F32)
    total = lax.dynamic_index_in_dim(acc, y, 0, keepdims=False)
    low = acc.astype(BF16)
    for d in (1, 2, 3):
        give = lax.dynamic_index_in_dim(low, (y + d) % 4, 0, keepdims=False)
        total = total + move_fsdp(give, dy=d).astype(F32)
    return total


def rounded(v):
    return lax.reduce_precision(v, 8, 7)


def sum_z(v):
    mine = rounded(v)
    other = move_ctx(mine.astype(BF16), dz=1)
    return rounded(mine + other.astype(F32)).astype(BF16)


def trans_dot(left, right):
    return lax.dot_general(
        left, right, (((0,), (0,)), ((), ())), preferred_element_type=F32
    )


def back_dot(left, right):
    return lax.dot_general(
        left, right, (((1,), (1,)), ((), ())), preferred_element_type=F32
    )


def plain_dot(left, right):
    return jnp.dot(left, right, preferred_element_type=F32)


def norm_scale(inputs):
    return lax.rsqrt(jnp.mean(inputs * inputs, axis=-1, keepdims=True) + EPSILON)


def norm_back(inputs, scales, gains, grads):
    weighted = grads * gains
    moment = jnp.mean(weighted * inputs, axis=-1, keepdims=True)
    return scales * weighted - inputs * scales * scales * scales * moment


def slot_of(j, x, zh):
    return (x - j // 2) % 4 + 4 * jnp.where(j % 2 == zh, 0, 1)


def attend_kernel(meta, q_ref, k_ref, v_ref, qs_ref, kid_ref, o_ref, ob_ref, l_ref):
    r = pl.program_id(0)
    x, zh = meta[0], meta[1]
    rows = q_ref.shape[2]
    q = q_ref[...].reshape(2 * rows, q_ref.shape[3])
    last = 2 * ((x - r) % 4) + zh
    qid = qs_ref[0, :, 0:1]
    start = qs_ref[0, :, 1:2]

    def step(j, acc):
        slot = slot_of(j, x, zh)
        s = back_dot(q, k_ref[slot])
        kid = kid_ref[slot]
        allowed = (kid <= qid) & (kid >= start)
        w = jnp.exp2(s * (SCALE * LOG2E)).reshape(2, rows, s.shape[1])
        w = jnp.where(allowed[None], w, 0.0).reshape(s.shape)
        return acc + plain_dot(w.astype(BF16), v_ref[slot])

    acc = lax.fori_loop(
        meta[2 + r], last + 1, step, jnp.zeros((2 * rows, v_ref.shape[2]), F32)
    )
    o = acc[:, :64] / acc[:, 64:65]
    o = jnp.concatenate([o[:rows], o[rows:]], axis=1)
    o_ref[0] = o
    ob_ref[0] = o.astype(BF16)
    l_ref[0] = acc.T[64:65]


def attend(meta, q, k, vx, qs, kid):
    rows = q.shape[2]
    full = lambda a: pl.BlockSpec(a.shape, lambda r, m: (0,) * a.ndim)
    return pl.pallas_call(
        attend_kernel,
        grid_spec=pltpu.PrefetchScalarGridSpec(
            num_scalar_prefetch=1,
            grid=(4,),
            in_specs=[
                pl.BlockSpec((2, 1, rows, 64), lambda r, m: (0, r, 0, 0)),
                full(k),
                full(vx),
                pl.BlockSpec((1, rows, 2), lambda r, m: (r, 0, 0)),
                full(kid),
            ],
            out_specs=[
                pl.BlockSpec((1, rows, 128), lambda r, m: (r, 0, 0)),
                pl.BlockSpec((1, rows, 128), lambda r, m: (r, 0, 0)),
                pl.BlockSpec((1, 1, 2 * rows), lambda r, m: (r, 0, 0)),
            ],
        ),
        out_shape=[
            jax.ShapeDtypeStruct((4, rows, 128), F32),
            jax.ShapeDtypeStruct((4, rows, 128), BF16),
            jax.ShapeDtypeStruct((4, 1, 2 * rows), F32),
        ],
        cost_estimate=pl.CostEstimate(
            flops=4_000_000_000, bytes_accessed=6_000_000, transcendentals=6_000_000
        ),
        name="attend",
    )(meta, q, k, vx, qs, kid)


def attend_back_kernel(
    meta, q_ref, do_ref, k_ref, v_ref, lse_ref, delta_ref, qs_ref, kid_ref,
    dq_ref, dk_ref, dv_ref,
):
    r = pl.program_id(0)
    x, zh = meta[0], meta[1]
    rows = q_ref.shape[2]
    q = q_ref[...].reshape(2 * rows, q_ref.shape[3])
    do = do_ref[0]
    do = jnp.concatenate([do[:, :64], do[:, 64:]], axis=0)
    last = 2 * ((x - r) % 4) + zh
    qid = qs_ref[0, 0:1]
    start = qs_ref[0, 1:2]
    lse = lse_ref[0]
    delta = delta_ref[0]

    @pl.when(r == 0)
    def _():
        dk_ref[...] = jnp.zeros_like(dk_ref)
        dv_ref[...] = jnp.zeros_like(dv_ref)

    def step(j, dq):
        slot = slot_of(j, x, zh)
        k = k_ref[slot]
        s = back_dot(k, q)
        kid = kid_ref[slot]
        allowed = (kid <= qid) & (kid >= start)
        p = jnp.where(allowed, jnp.exp2(s * (SCALE * LOG2E) - lse), 0.0)
        dp = back_dot(v_ref[slot], do)
        ds = (p * (dp - delta)).astype(BF16)
        dk_ref[slot] += plain_dot(ds, q)
        dv_ref[slot] += plain_dot(p.astype(BF16), do)
        return dq + trans_dot(ds, k)

    dq = lax.fori_loop(
        meta[2 + r], last + 1, step, jnp.zeros((2 * rows, 64), F32)
    )
    dq_ref[...] = (dq * SCALE).reshape(dq_ref.shape)


def attend_back(meta, q, do, k, v, lse, delta, qs, kid):
    rows = q.shape[2]
    full = lambda a: pl.BlockSpec(a.shape, lambda r, m: (0,) * a.ndim)
    row = lambda n: pl.BlockSpec((1, n, 2 * rows), lambda r, m: (r, 0, 0))
    return pl.pallas_call(
        attend_back_kernel,
        grid_spec=pltpu.PrefetchScalarGridSpec(
            num_scalar_prefetch=1,
            grid=(4,),
            in_specs=[
                pl.BlockSpec((2, 1, rows, 64), lambda r, m: (0, r, 0, 0)),
                pl.BlockSpec((1, rows, 128), lambda r, m: (r, 0, 0)),
                full(k),
                full(v),
                row(1),
                row(1),
                row(2),
                full(kid),
            ],
            out_specs=[
                pl.BlockSpec((2, 1, rows, 64), lambda r, m: (0, r, 0, 0)),
                pl.BlockSpec(k.shape, lambda r, m: (0, 0, 0)),
                pl.BlockSpec(k.shape, lambda r, m: (0, 0, 0)),
            ],
        ),
        out_shape=[
            jax.ShapeDtypeStruct(q.shape, F32),
            jax.ShapeDtypeStruct(k.shape, F32),
            jax.ShapeDtypeStruct(k.shape, F32),
        ],
        cost_estimate=pl.CostEstimate(
            flops=10_000_000_000, bytes_accessed=9_000_000, transcendentals=6_000_000
        ),
        name="attend_back",
    )(meta, q, do, k, v, lse, delta, qs, kid)


def local(
    tokens, positions, cotangent, attn_gain, w_query, w_key, w_value, query_gain,
    key_gain, w_out, ffn_gain, w_gate, w_up, w_down,
):
    ctx, fsdp = lax.axis_index("ctx"), lax.axis_index("fsdp")
    x, zh, c = ctx // 4, (ctx // 2) % 2, ctx % 2
    t = x * 2 + c
    y, zl = fsdp // 2, fsdp % 2
    first = c == 0
    rows = tokens.shape[1]
    width = tokens.shape[2]
    part_rows = w_query.shape[0]
    hidden_all = w_gate.shape[1]
    hid = hidden_all // 8
    toks = 8 * rows

    def half(w, size):
        both = lax.dynamic_slice_in_dim(w, x * (2 * size), 2 * size, 1)
        return jnp.where(first, both[:, :size], both[:, size:])

    pos = positions[0]
    pos_rows = jnp.stack([pos // 64, pos % 64]).astype(F32).astype(BF16)
    pos_rows = jnp.pad(pos_rows, ((0, 14), (0, width - rows)))
    packed = jnp.concatenate([tokens[0], pos_rows], axis=0)
    blocks = gather_group(packed)
    gains = jnp.concatenate([attn_gain, ffn_gain])[None]
    small = jnp.concatenate([query_gain, key_gain, jnp.zeros((240,), BF16)])[None]
    piece = jnp.concatenate(
        [
            jnp.concatenate([half(w_query, 128), half(w_key, 64), half(w_value, 64)], axis=1),
            gains,
            small,
            jnp.zeros((14, 256), BF16),
        ],
        axis=0,
    )
    got = gather_fsdp(piece, y, zl)
    w_qkv = got[:, :part_rows].reshape(width, 256)
    norm_attn = got[:, part_rows, :part_rows].reshape(width).astype(F32)
    norm_ffn = got[:, part_rows, part_rows:].reshape(width).astype(F32)
    norm_query = got[:, part_rows + 1, :8].reshape(64).astype(F32)
    norm_key = got[:, part_rows + 1, 8:16].reshape(64).astype(F32)
    out_cols = gather_fsdp(half(w_out, 128), y, zl).reshape(width, 128)
    full_out = jnp.zeros((width, width), BF16)
    for r, pair in enumerate(gather_group(out_cols)):
        both = jnp.concatenate(
            [jnp.where(first, pair[0], pair[1]), jnp.where(first, pair[1], pair[0])], axis=1
        )
        full_out = lax.dynamic_update_slice_in_dim(full_out, both, ((x - r) % 4) * 256, 1)
    gate_up = jnp.concatenate([half(w_gate, hid), half(w_up, hid)], axis=1)
    gate_up = gather_fsdp(gate_up, y, zl).reshape(width, 2 * hid)
    w_gate_t, w_up_t = gate_up[:, :hid], gate_up[:, hid:]
    down_rows = hid // 8
    down = swap_roles(lax.dynamic_slice_in_dim(w_down, t * down_rows, down_rows, 0))
    w_down_t = gather_fsdp(down, y, zl).reshape(hid, width)
    grad_output = joined(gather_group(cotangent[0]))

    x_all = jnp.concatenate([b[:rows] for pair in blocks for b in pair], axis=0)
    pos_hi = jnp.concatenate([b[rows, :rows] for pair in blocks for b in pair])
    pos_lo = jnp.concatenate([b[rows + 1, :rows] for pair in blocks for b in pair])
    token_pos = (pos_hi.astype(F32) * 64.0 + pos_lo.astype(F32)).astype(jnp.int32)
    x_float = x_all.astype(F32)
    normed = (x_float * norm_scale(x_float) * norm_attn).astype(BF16)
    qkv = plain_dot(normed, w_qkv)
    raw = jnp.stack([qkv[:, 0:64], qkv[:, 64:128], qkv[:, 128:192]])
    value_low = qkv[:, 192:].astype(BF16)
    scale_raw = norm_scale(raw)
    gain_raw = jnp.stack([norm_query, norm_query, norm_key])[:, None, :]
    frequency = ROPE_BASE ** (-(jnp.arange(32, dtype=F32) * 2.0 / 64))
    angles = token_pos.astype(F32)[:, None] * frequency[None, :]
    cosines, sines = jnp.cos(angles), jnp.sin(angles)
    cos_all = jnp.concatenate([cosines, cosines], axis=1)
    sin_all = jnp.concatenate([sines, sines], axis=1)
    normal = raw * scale_raw * gain_raw
    turned = jnp.concatenate([-normal[..., 32:], normal[..., :32]], axis=-1)
    rot = (normal * cos_all + turned * sin_all).astype(BF16)
    query_rot = rot[:2].reshape(2, 4, 2 * rows, 64)
    pair_home = jnp.concatenate([rot[2], value_low], axis=1)
    pair_away = move_ctx(pair_home, dz=1)
    pairs = jnp.concatenate([pair_home, pair_away]).reshape(8, 2 * rows, 128)
    keys = pairs[..., :64]
    values = pairs[..., 64:]
    values_one = jnp.concatenate(
        [values, jnp.ones((8, 2 * rows, 1), BF16), jnp.zeros((8, 2 * rows, 63), BF16)], axis=-1
    )
    chips = (x - jnp.arange(4, dtype=jnp.int32)) % 4
    cores = jnp.stack([c, 1 - c]).astype(jnp.int32)
    base = (chips * 4)[:, None] + cores[None, :]
    inner = jnp.arange(rows, dtype=jnp.int32)
    ids = lambda z: ((base + 2 * z)[:, :, None] * rows + inner).reshape(4, 2 * rows)
    query_ids = ids(zh)
    key_ids = jnp.concatenate([query_ids, ids(1 - zh)])
    start_ids = query_ids - token_pos.reshape(4, 2 * rows)
    lowest = jnp.maximum(jnp.min(start_ids, axis=1), 0) // (2 * rows)
    meta = jnp.concatenate([jnp.stack([x, zh]), lowest]).astype(jnp.int32)
    attn_float, attn_part, row_total = attend(
        meta,
        query_rot,
        keys,
        values_one,
        jnp.stack([query_ids, start_ids], axis=-1),
        key_ids[:, None, :],
    )

    part4 = attn_part.reshape(4, 2, rows, 128)
    arrived = exchange_group([[part4[r, 0], part4[r, 1]] for r in range(4)])
    attn_low = jnp.zeros((rows, width), BF16)
    for r in range(4):
        own, oth = arrived[r]
        both = jnp.concatenate([jnp.where(first, own, oth), jnp.where(first, oth, own)], axis=1)
        attn_low = lax.dynamic_update_slice_in_dim(attn_low, both, ((x + r) % 4) * 256, 1)
    x_own = tokens[0].astype(F32)
    hidden = x_own + plain_dot(attn_low, full_out)
    scale_ffn = norm_scale(hidden)
    mlp_own = (hidden * scale_ffn * norm_ffn).astype(BF16)

    mlp_input = joined(gather_group(mlp_own))
    gate_proj = plain_dot(mlp_input, w_gate_t)
    up_proj = plain_dot(mlp_input, w_up_t)
    grad_mlp = back_dot(grad_output, w_down_t)
    gate_sigmoid = jax.nn.sigmoid(gate_proj)
    mlp_hidden = (gate_proj * gate_sigmoid * up_proj).astype(BF16)
    grad_gate_low = (
        grad_mlp * up_proj * gate_sigmoid * (1.0 + gate_proj * (1.0 - gate_sigmoid))
    ).astype(BF16)
    grad_up_low = (grad_mlp * gate_proj * gate_sigmoid).astype(BF16)
    grad_in_part = back_dot(grad_gate_low, w_gate_t) + back_dot(grad_up_low, w_up_t)
    split = lambda v: v.reshape((4, 2, rows) + v.shape[1:])
    grad_mlp_input = scatter_group(split(grad_in_part.astype(BF16)))
    grad_hidden = cotangent[0].astype(F32) + norm_back(
        hidden, scale_ffn, norm_ffn, grad_mlp_input
    )
    hidden_low = grad_hidden.astype(BF16)
    grad_attn_own = back_dot(hidden_low, full_out).astype(BF16)

    def head_block(r, s):
        pair = lax.dynamic_slice_in_dim(grad_attn_own, ((x - r) % 4) * 256, 256, 1)
        swap = first if s == 0 else jnp.logical_not(first)
        return jnp.where(swap, pair[:, :128], pair[:, 128:])

    arrived = exchange_group([[head_block(r, s) for s in range(2)] for r in range(4)])
    grad_attn = joined([arrived[(4 - r) % 4] for r in range(4)]).reshape(4, 2 * rows, 128)
    delta = grad_attn.astype(F32) * attn_float
    row_delta = jnp.stack(
        [jnp.sum(delta[..., :64], axis=-1), jnp.sum(delta[..., 64:], axis=-1)], axis=1
    ).reshape(4, 1, 4 * rows)
    twice = lambda v: jnp.concatenate([v, v], axis=-1)
    grad_query, grad_key, grad_value = attend_back(
        meta,
        query_rot,
        grad_attn,
        keys,
        values,
        jnp.log2(row_total),
        row_delta,
        jnp.stack([twice(query_ids), twice(start_ids)], axis=1),
        key_ids[:, :, None],
    )
    pair_grad = jnp.concatenate([grad_key * SCALE, grad_value], axis=-1)
    away = move_ctx(pair_grad[4:].astype(BF16), dz=1)
    pair_grad = (pair_grad[:4] + away.astype(F32)).reshape(toks, 128)
    grad_rot = jnp.concatenate([grad_query.reshape(2, toks, 64), pair_grad[None, :, :64]])
    turned = jnp.concatenate([grad_rot[..., 32:], -grad_rot[..., :32]], axis=-1)
    grad_normal = grad_rot * cos_all + turned * sin_all
    gain_sums = jnp.sum(grad_normal * raw * scale_raw, axis=1)
    raw_back = norm_back(raw, scale_raw, gain_raw, grad_normal).astype(BF16)
    qkv_back = jnp.concatenate(
        [raw_back[0], raw_back[1], raw_back[2], pair_grad[:, 64:].astype(BF16)], axis=1
    )
    grad_normed = scatter_group(split(back_dot(qkv_back, w_qkv).astype(BF16)))
    scale_own = norm_scale(x_own)
    grad_tokens = (
        grad_hidden + norm_back(x_own, scale_own, norm_attn, grad_normed)
    ).astype(BF16)

    result = scatter_group(split(plain_dot(mlp_hidden, w_down_t).astype(BF16)))
    result = (hidden + result).astype(BF16)

    grad_down = trans_dot(mlp_hidden, grad_output)
    grad_gate_w = trans_dot(mlp_input, grad_gate_low)
    grad_up_w = trans_dot(mlp_input, grad_up_low)
    sum_ffn_gain = (
        jnp.sum(grad_gate_w * w_gate_t.astype(F32), axis=1)
        + jnp.sum(grad_up_w * w_up_t.astype(F32), axis=1)
    ) / norm_ffn
    grad_gu = jnp.concatenate([grad_gate_w.astype(BF16), grad_up_w.astype(BF16)], axis=1)
    piece_gu = sum_z(scatter_fsdp(grad_gu.reshape(8, part_rows, 2 * hid), y, zl))
    piece_down = sum_z(scatter_fsdp(grad_down.astype(BF16).reshape(8, down_rows, width), y, zl))
    piece_down = swap_roles(piece_down)

    grad_out_w = trans_dot(attn_low, hidden_low).astype(BF16)

    def out_block(r, s):
        pair = lax.dynamic_slice_in_dim(grad_out_w, ((x - r) % 4) * 256, 256, 1)
        swap = first if s == 0 else jnp.logical_not(first)
        return jnp.where(swap, pair[:, :128], pair[:, 128:])

    grad_out_t = scatter_group(
        jnp.stack([jnp.stack([out_block(r, s) for s in range(2)]) for r in range(4)])
    )
    piece_out = sum_z(scatter_fsdp(grad_out_t.astype(BF16).reshape(8, part_rows, 128), y, zl))

    grad_qkv_w = trans_dot(normed, qkv_back)
    sum_attn_gain = jnp.sum(grad_qkv_w * w_qkv.astype(F32), axis=1) / norm_attn
    gain_rows = jnp.concatenate(
        [sum_attn_gain.reshape(8, 1, part_rows), sum_ffn_gain.reshape(8, 1, part_rows)], axis=2
    )
    small_rows = jnp.concatenate(
        [
            (gain_sums[0] + gain_sums[1]).reshape(8, 1, 8),
            gain_sums[2].reshape(8, 1, 8),
            jnp.zeros((8, 1, 240), F32),
        ],
        axis=2,
    )
    piece_qkv = jnp.concatenate(
        [
            grad_qkv_w.reshape(8, part_rows, 256),
            gain_rows,
            small_rows,
            jnp.zeros((8, 14, 256), F32),
        ],
        axis=1,
    )
    piece_qkv = sum_z(scatter_fsdp(piece_qkv.astype(BF16), y, zl))

    def in_order(piece):
        for r, (own, oth) in enumerate(gather_group(piece)):
            yield r, jnp.where(first, own, oth), jnp.where(first, oth, own)

    def columns(pieces, size):
        full = jnp.zeros((part_rows, 8 * size), F32)
        for r, one, two in pieces:
            both = jnp.concatenate([one, two], axis=1).astype(F32)
            full = lax.dynamic_update_slice_in_dim(full, both, ((x - r) % 4) * (2 * size), 1)
        return full

    gu = list(in_order(piece_gu))
    total_gate = columns([(r, a[:, :hid], b[:, :hid]) for r, a, b in gu], hid)
    total_up = columns([(r, a[:, hid:], b[:, hid:]) for r, a, b in gu], hid)
    total_down = jnp.zeros(w_down.shape, F32)
    for r, a, b in in_order(piece_down):
        total_down = lax.dynamic_update_slice_in_dim(
            total_down,
            jnp.concatenate([a, b]).astype(F32),
            ((x - r) % 4) * (2 * down_rows),
            0,
        )
    total_out = columns(in_order(piece_out), 128)
    qkv_pieces = list(in_order(piece_qkv))
    rows_of = slice(0, part_rows)
    total_query = columns([(r, a[rows_of, :128], b[rows_of, :128]) for r, a, b in qkv_pieces], 128)
    total_key = columns([(r, a[rows_of, 128:192], b[rows_of, 128:192]) for r, a, b in qkv_pieces], 64)
    total_value = columns([(r, a[rows_of, 192:], b[rows_of, 192:]) for r, a, b in qkv_pieces], 64)
    extra = jnp.zeros((8, 2, 256), F32)
    for r, a, b in qkv_pieces:
        both = jnp.stack([a[part_rows : part_rows + 2], b[part_rows : part_rows + 2]]).astype(F32)
        extra = lax.dynamic_update_slice_in_dim(extra, both, ((x - r) % 4) * 2, 0)
    extra = jnp.sum(extra, axis=0)
    return (
        result[None],
        grad_tokens[None],
        extra[0, :part_rows],
        total_query,
        total_key,
        total_value,
        extra[1, :8],
        extra[1, 8:16],
        total_out,
        extra[0, part_rows:],
        total_gate,
        total_up,
        total_down,
    )


def solution(mesh):
    tok, vec, mat = P("fsdp", "ctx", None), P("fsdp"), P("fsdp", None)
    return jax.shard_map(
        local,
        mesh=mesh,
        in_specs=(
            tok, P("fsdp", "ctx"), tok, vec, mat, mat, mat, vec, vec, mat, vec, mat, mat, mat,
        ),
        out_specs=(tok, tok, vec, mat, mat, mat, vec, vec, mat, vec, mat, mat, mat),
        check_vma=False,
    )
```

```python
import functools

import jax
import jax.numpy as jnp
from jax import lax
from jax.experimental import pallas as pl
from jax.experimental.pallas import tpu as pltpu
from jax.sharding import PartitionSpec as P

EPSILON = 1e-05
ROPE_BASE = 1000000.0
F32 = jnp.float32
BF16 = jnp.bfloat16
LOG2E = 1.4426950408889634
SCALE = 0.125


def move_ctx(v, dx=0, dz=0, dc=0):
    pairs = [
        (a * 4 + b * 2 + c, ((a + dx) % 4) * 4 + (b ^ dz) * 2 + (c ^ dc))
        for a in range(4)
        for b in range(2)
        for c in range(2)
    ]
    return lax.ppermute(v, "ctx", pairs)


def move_fsdp(v, dy=0, dz=0):
    pairs = [
        (a * 2 + b, ((a + dy) % 4) * 2 + (b ^ dz)) for a in range(4) for b in range(2)
    ]
    return lax.ppermute(v, "fsdp", pairs)


def swap_roles(v):
    pairs = []
    for t in range(8):
        for h in range(2):
            for f in range(8):
                src = ((t // 2) * 4 + h * 2 + t % 2) * 8 + f
                dst = ((f // 2) * 4 + h * 2 + f % 2) * 8 + t
                pairs.append((src, dst))
    return lax.ppermute(v, ("ctx", "fsdp"), pairs)


def gather_group(u):
    home = move_ctx(u, dc=1)
    away = jnp.stack([move_ctx(u, dx=1), move_ctx(u, dx=2), move_ctx(u, dx=3)])
    other = move_ctx(away, dc=1)
    return [[u, home]] + [[away[r], other[r]] for r in range(3)]


def joined(blocks):
    return jnp.concatenate([b for pair in blocks for b in pair], axis=0)


def scatter_group(part):
    other = move_ctx(part[1:, 1].astype(BF16), dc=1)
    other_home = move_ctx(part[0, 1].astype(BF16), dc=1)
    total = part[0, 0].astype(F32) + other_home.astype(F32)
    for r in (1, 2, 3):
        acc = part[r, 0].astype(F32) + other[r - 1].astype(F32)
        total = total + move_ctx(acc.astype(BF16), dx=-r).astype(F32)
    return total


def exchange_group(blocks):
    other = move_ctx(jnp.stack([blocks[r][1] for r in range(4)]), dc=1)
    out = [[blocks[0][0], other[0]]]
    for r in (1, 2, 3):
        both = move_ctx(jnp.stack([blocks[r][0], other[r]]), dx=-r)
        out.append([both[0], both[1]])
    return out


def gather_fsdp(u, y, zl):
    o = move_fsdp(u, dz=1)
    low = zl == 0
    pair = jnp.stack([jnp.where(low, u, o), jnp.where(low, o, u)])
    full = jnp.zeros((4,) + pair.shape, u.dtype)
    for d in range(4):
        got = pair if d == 0 else move_fsdp(pair, dy=d)
        full = lax.dynamic_update_index_in_dim(full, got, (y - d) % 4, 0)
    return full.reshape((8,) + u.shape)


def scatter_fsdp(part, y, zl):
    part = part.reshape((4, 2) + part.shape[1:])
    low = zl == 0
    give = jnp.where(low, part[:, 1], part[:, 0]).astype(BF16)
    keep = jnp.where(low, part[:, 0], part[:, 1])
    acc = keep.astype(F32) + move_fsdp(give, dz=1).astype(F32)
    total = lax.dynamic_index_in_dim(acc, y, 0, keepdims=False)
    low = acc.astype(BF16)
    for d in (1, 2, 3):
        give = lax.dynamic_index_in_dim(low, (y + d) % 4, 0, keepdims=False)
        total = total + move_fsdp(give, dy=d).astype(F32)
    return total


def rounded(v):
    return lax.reduce_precision(v, 8, 7)


def sum_z(v):
    mine = rounded(v)
    other = move_ctx(mine.astype(BF16), dz=1)
    return rounded(mine + other.astype(F32)).astype(BF16)


def trans_dot(left, right):
    return lax.dot_general(
        left, right, (((0,), (0,)), ((), ())), preferred_element_type=F32
    )


def back_dot(left, right):
    return lax.dot_general(
        left, right, (((1,), (1,)), ((), ())), preferred_element_type=F32
    )


def plain_dot(left, right):
    return jnp.dot(left, right, preferred_element_type=F32)


def norm_scale(inputs):
    return lax.rsqrt(jnp.mean(inputs * inputs, axis=-1, keepdims=True) + EPSILON)


def norm_back(inputs, scales, gains, grads):
    weighted = grads * gains
    moment = jnp.mean(weighted * inputs, axis=-1, keepdims=True)
    return scales * weighted - inputs * scales * scales * scales * moment


def slot_of(j, x, zh):
    return (x - j // 2) % 4 + 4 * jnp.where(j % 2 == zh, 0, 1)


def attend_kernel(meta, q_ref, k_ref, v_ref, qs_ref, kid_ref, o_ref, ob_ref, l_ref):
    r = pl.program_id(0)
    x, zh = meta[0], meta[1]
    rows = q_ref.shape[2]
    q = q_ref[...].reshape(2 * rows, q_ref.shape[3])
    last = 2 * ((x - r) % 4) + zh
    qid = qs_ref[0, :, 0:1]
    start = qs_ref[0, :, 1:2]

    def step(j, acc):
        slot = slot_of(j, x, zh)
        s = back_dot(q, k_ref[slot])
        kid = kid_ref[slot]
        allowed = (kid <= qid) & (kid >= start)
        w = jnp.exp2(s * (SCALE * LOG2E)).reshape(2, rows, s.shape[1])
        w = jnp.where(allowed[None], w, 0.0).reshape(s.shape)
        return acc + plain_dot(w.astype(BF16), v_ref[slot])

    acc = lax.fori_loop(
        meta[2 + r], last + 1, step, jnp.zeros((2 * rows, v_ref.shape[2]), F32)
    )
    o = acc[:, :64] / acc[:, 64:65]
    o = jnp.concatenate([o[:rows], o[rows:]], axis=1)
    o_ref[0] = o
    ob_ref[0] = o.astype(BF16)
    l_ref[0] = acc.T[64:65]


def attend(meta, q, k, vx, qs, kid):
    rows = q.shape[2]
    full = lambda a: pl.BlockSpec(a.shape, lambda r, m: (0,) * a.ndim)
    return pl.pallas_call(
        attend_kernel,
        grid_spec=pltpu.PrefetchScalarGridSpec(
            num_scalar_prefetch=1,
            grid=(4,),
            in_specs=[
                pl.BlockSpec((2, 1, rows, 64), lambda r, m: (0, r, 0, 0)),
                full(k),
                full(vx),
                pl.BlockSpec((1, rows, 2), lambda r, m: (r, 0, 0)),
                full(kid),
            ],
            out_specs=[
                pl.BlockSpec((1, rows, 128), lambda r, m: (r, 0, 0)),
                pl.BlockSpec((1, rows, 128), lambda r, m: (r, 0, 0)),
                pl.BlockSpec((1, 1, 2 * rows), lambda r, m: (r, 0, 0)),
            ],
        ),
        out_shape=[
            jax.ShapeDtypeStruct((4, rows, 128), F32),
            jax.ShapeDtypeStruct((4, rows, 128), BF16),
            jax.ShapeDtypeStruct((4, 1, 2 * rows), F32),
        ],
        cost_estimate=pl.CostEstimate(
            flops=4_000_000_000, bytes_accessed=6_000_000, transcendentals=6_000_000
        ),
        name="attend",
    )(meta, q, k, vx, qs, kid)


def attend_back_kernel(
    meta, q_ref, do_ref, k_ref, v_ref, lse_ref, delta_ref, qs_ref, kid_ref,
    dq_ref, dk_ref, dv_ref,
):
    r = pl.program_id(0)
    x, zh = meta[0], meta[1]
    rows = q_ref.shape[2]
    q = q_ref[...].reshape(2 * rows, q_ref.shape[3])
    do = do_ref[0]
    do = jnp.concatenate([do[:, :64], do[:, 64:]], axis=0)
    last = 2 * ((x - r) % 4) + zh
    qid = qs_ref[0, 0:1]
    start = qs_ref[0, 1:2]
    lse = lse_ref[0]
    delta = delta_ref[0]

    @pl.when(r == 0)
    def _():
        dk_ref[...] = jnp.zeros_like(dk_ref)
        dv_ref[...] = jnp.zeros_like(dv_ref)

    def step(j, dq):
        slot = slot_of(j, x, zh)
        k = k_ref[slot]
        s = back_dot(k, q)
        kid = kid_ref[slot]
        allowed = (kid <= qid) & (kid >= start)
        p = jnp.where(allowed, jnp.exp2(s * (SCALE * LOG2E) - lse), 0.0)
        dp = back_dot(v_ref[slot], do)
        ds = (p * (dp - delta)).astype(BF16)
        dk_ref[slot] += plain_dot(ds, q)
        dv_ref[slot] += plain_dot(p.astype(BF16), do)
        return dq + trans_dot(ds, k)

    dq = lax.fori_loop(
        meta[2 + r], last + 1, step, jnp.zeros((2 * rows, 64), F32)
    )
    dq_ref[...] = (dq * SCALE).reshape(dq_ref.shape)


def attend_back(meta, q, do, k, v, lse, delta, qs, kid):
    rows = q.shape[2]
    full = lambda a: pl.BlockSpec(a.shape, lambda r, m: (0,) * a.ndim)
    row = lambda n: pl.BlockSpec((1, n, 2 * rows), lambda r, m: (r, 0, 0))
    return pl.pallas_call(
        attend_back_kernel,
        grid_spec=pltpu.PrefetchScalarGridSpec(
            num_scalar_prefetch=1,
            grid=(4,),
            in_specs=[
                pl.BlockSpec((2, 1, rows, 64), lambda r, m: (0, r, 0, 0)),
                pl.BlockSpec((1, rows, 128), lambda r, m: (r, 0, 0)),
                full(k),
                full(v),
                row(1),
                row(1),
                row(2),
                full(kid),
            ],
            out_specs=[
                pl.BlockSpec((2, 1, rows, 64), lambda r, m: (0, r, 0, 0)),
                pl.BlockSpec(k.shape, lambda r, m: (0, 0, 0)),
                pl.BlockSpec(k.shape, lambda r, m: (0, 0, 0)),
            ],
        ),
        out_shape=[
            jax.ShapeDtypeStruct(q.shape, F32),
            jax.ShapeDtypeStruct(k.shape, F32),
            jax.ShapeDtypeStruct(k.shape, F32),
        ],
        cost_estimate=pl.CostEstimate(
            flops=10_000_000_000, bytes_accessed=9_000_000, transcendentals=6_000_000
        ),
        name="attend_back",
    )(meta, q, do, k, v, lse, delta, qs, kid)


def local(
    tokens, positions, cotangent, attn_gain, w_query, w_key, w_value, query_gain,
    key_gain, w_out, ffn_gain, w_gate, w_up, w_down,
):
    ctx, fsdp = lax.axis_index("ctx"), lax.axis_index("fsdp")
    x, zh, c = ctx // 4, (ctx // 2) % 2, ctx % 2
    t = x * 2 + c
    y, zl = fsdp // 2, fsdp % 2
    first = c == 0
    rows = tokens.shape[1]
    width = tokens.shape[2]
    part_rows = w_query.shape[0]
    hidden_all = w_gate.shape[1]
    hid = hidden_all // 8
    toks = 8 * rows

    def half(w, size):
        both = lax.dynamic_slice_in_dim(w, x * (2 * size), 2 * size, 1)
        return jnp.where(first, both[:, :size], both[:, size:])

    pos = positions[0]
    pos_rows = jnp.stack([pos // 64, pos % 64]).astype(F32).astype(BF16)
    pos_rows = jnp.pad(pos_rows, ((0, 14), (0, width - rows)))
    packed = jnp.concatenate([tokens[0], pos_rows], axis=0)
    blocks = gather_group(packed)
    gains = jnp.concatenate([attn_gain, ffn_gain])[None]
    small = jnp.concatenate([query_gain, key_gain, jnp.zeros((240,), BF16)])[None]
    piece = jnp.concatenate(
        [
            jnp.concatenate([half(w_query, 128), half(w_key, 64), half(w_value, 64)], axis=1),
            gains,
            small,
            jnp.zeros((14, 256), BF16),
        ],
        axis=0,
    )
    got = gather_fsdp(piece, y, zl)
    w_qkv = got[:, :part_rows].reshape(width, 256)
    norm_attn = got[:, part_rows, :part_rows].reshape(width).astype(F32)
    norm_ffn = got[:, part_rows, part_rows:].reshape(width).astype(F32)
    norm_query = got[:, part_rows + 1, :8].reshape(64).astype(F32)
    norm_key = got[:, part_rows + 1, 8:16].reshape(64).astype(F32)
    gate_up = jnp.concatenate(
        [half(w_gate, hid), half(w_up, hid), half(w_out, 128)], axis=1
    )
    gate_up = gather_fsdp(gate_up, y, zl).reshape(width, 2 * hid + 128)
    gate_up, out_cols = gate_up[:, : 2 * hid], gate_up[:, 2 * hid :]
    full_out = jnp.zeros((width, width), BF16)
    for r, pair in enumerate(gather_group(out_cols)):
        both = jnp.concatenate(
            [jnp.where(first, pair[0], pair[1]), jnp.where(first, pair[1], pair[0])], axis=1
        )
        full_out = lax.dynamic_update_slice_in_dim(full_out, both, ((x - r) % 4) * 256, 1)
    down_rows = hid // 8
    down = swap_roles(lax.dynamic_slice_in_dim(w_down, t * down_rows, down_rows, 0))
    w_down_t = gather_fsdp(down, y, zl).reshape(hid, width)
    grad_output = joined(gather_group(cotangent[0]))

    x_all = jnp.concatenate([b[:rows] for pair in blocks for b in pair], axis=0)
    pos_hi = jnp.concatenate([b[rows, :rows] for pair in blocks for b in pair])
    pos_lo = jnp.concatenate([b[rows + 1, :rows] for pair in blocks for b in pair])
    token_pos = (pos_hi.astype(F32) * 64.0 + pos_lo.astype(F32)).astype(jnp.int32)
    x_float = x_all.astype(F32)
    normed = (x_float * norm_scale(x_float) * norm_attn).astype(BF16)
    qkv = plain_dot(normed, w_qkv)
    raw = jnp.stack([qkv[:, 0:64], qkv[:, 64:128], qkv[:, 128:192]])
    value_low = qkv[:, 192:].astype(BF16)
    scale_raw = norm_scale(raw)
    gain_raw = jnp.stack([norm_query, norm_query, norm_key])[:, None, :]
    frequency = ROPE_BASE ** (-(jnp.arange(32, dtype=F32) * 2.0 / 64))
    angles = token_pos.astype(F32)[:, None] * frequency[None, :]
    cosines, sines = jnp.cos(angles), jnp.sin(angles)
    cos_all = jnp.concatenate([cosines, cosines], axis=1)
    sin_all = jnp.concatenate([sines, sines], axis=1)
    normal = raw * scale_raw * gain_raw
    turned = jnp.concatenate([-normal[..., 32:], normal[..., :32]], axis=-1)
    rot = (normal * cos_all + turned * sin_all).astype(BF16)
    query_rot = rot[:2].reshape(2, 4, 2 * rows, 64)
    pair_home = jnp.concatenate([rot[2], value_low], axis=1)
    pair_away = move_ctx(pair_home, dz=1)
    pairs = jnp.concatenate([pair_home, pair_away]).reshape(8, 2 * rows, 128)
    keys = pairs[..., :64]
    values = pairs[..., 64:]
    values_one = jnp.concatenate(
        [values, jnp.ones((8, 2 * rows, 1), BF16), jnp.zeros((8, 2 * rows, 63), BF16)], axis=-1
    )
    chips = (x - jnp.arange(4, dtype=jnp.int32)) % 4
    cores = jnp.stack([c, 1 - c]).astype(jnp.int32)
    base = (chips * 4)[:, None] + cores[None, :]
    inner = jnp.arange(rows, dtype=jnp.int32)
    ids = lambda z: ((base + 2 * z)[:, :, None] * rows + inner).reshape(4, 2 * rows)
    query_ids = ids(zh)
    key_ids = jnp.concatenate([query_ids, ids(1 - zh)])
    start_ids = query_ids - token_pos.reshape(4, 2 * rows)
    lowest = jnp.maximum(jnp.min(start_ids, axis=1), 0) // (2 * rows)
    meta = jnp.concatenate([jnp.stack([x, zh]), lowest]).astype(jnp.int32)
    attn_float, attn_part, row_total = attend(
        meta,
        query_rot,
        keys,
        values_one,
        jnp.stack([query_ids, start_ids], axis=-1),
        key_ids[:, None, :],
    )

    part4 = attn_part.reshape(4, 2, rows, 128)
    arrived = exchange_group([[part4[r, 0], part4[r, 1]] for r in range(4)])
    attn_low = jnp.zeros((rows, width), BF16)
    for r in range(4):
        own, oth = arrived[r]
        both = jnp.concatenate([jnp.where(first, own, oth), jnp.where(first, oth, own)], axis=1)
        attn_low = lax.dynamic_update_slice_in_dim(attn_low, both, ((x + r) % 4) * 256, 1)
    x_own = tokens[0].astype(F32)
    hidden = x_own + plain_dot(attn_low, full_out)
    scale_ffn = norm_scale(hidden)
    mlp_own = (hidden * scale_ffn * norm_ffn).astype(BF16)

    mlp_input = joined(gather_group(mlp_own))
    both_proj = plain_dot(mlp_input, gate_up)
    gate_proj, up_proj = both_proj[:, :hid], both_proj[:, hid:]
    grad_mlp = back_dot(grad_output, w_down_t)
    gate_sigmoid = jax.nn.sigmoid(gate_proj)
    mlp_hidden = (gate_proj * gate_sigmoid * up_proj).astype(BF16)
    grad_gate_low = (
        grad_mlp * up_proj * gate_sigmoid * (1.0 + gate_proj * (1.0 - gate_sigmoid))
    ).astype(BF16)
    grad_up_low = (grad_mlp * gate_proj * gate_sigmoid).astype(BF16)
    grad_both_low = jnp.concatenate([grad_gate_low, grad_up_low], axis=1)
    grad_in_part = back_dot(grad_both_low, gate_up)
    split = lambda v: v.reshape((4, 2, rows) + v.shape[1:])
    grad_mlp_input = scatter_group(split(grad_in_part.astype(BF16)))
    grad_hidden = cotangent[0].astype(F32) + norm_back(
        hidden, scale_ffn, norm_ffn, grad_mlp_input
    )
    hidden_low = grad_hidden.astype(BF16)
    grad_attn_own = back_dot(hidden_low, full_out).astype(BF16)

    def head_block(r, s):
        pair = lax.dynamic_slice_in_dim(grad_attn_own, ((x - r) % 4) * 256, 256, 1)
        swap = first if s == 0 else jnp.logical_not(first)
        return jnp.where(swap, pair[:, :128], pair[:, 128:])

    arrived = exchange_group([[head_block(r, s) for s in range(2)] for r in range(4)])
    grad_attn = joined([arrived[(4 - r) % 4] for r in range(4)]).reshape(4, 2 * rows, 128)
    delta = grad_attn.astype(F32) * attn_float
    row_delta = jnp.stack(
        [jnp.sum(delta[..., :64], axis=-1), jnp.sum(delta[..., 64:], axis=-1)], axis=1
    ).reshape(4, 1, 4 * rows)
    twice = lambda v: jnp.concatenate([v, v], axis=-1)
    grad_query, grad_key, grad_value = attend_back(
        meta,
        query_rot,
        grad_attn,
        keys,
        values,
        jnp.log2(row_total),
        row_delta,
        jnp.stack([twice(query_ids), twice(start_ids)], axis=1),
        key_ids[:, :, None],
    )
    pair_grad = jnp.concatenate([grad_key * SCALE, grad_value], axis=-1)
    away = move_ctx(pair_grad[4:].astype(BF16), dz=1)
    pair_grad = (pair_grad[:4] + away.astype(F32)).reshape(toks, 128)
    grad_rot = jnp.concatenate([grad_query.reshape(2, toks, 64), pair_grad[None, :, :64]])
    turned = jnp.concatenate([grad_rot[..., 32:], -grad_rot[..., :32]], axis=-1)
    grad_normal = grad_rot * cos_all + turned * sin_all
    gain_sums = jnp.sum(grad_normal * raw * scale_raw, axis=1)
    raw_back = norm_back(raw, scale_raw, gain_raw, grad_normal).astype(BF16)
    qkv_back = jnp.concatenate(
        [raw_back[0], raw_back[1], raw_back[2], pair_grad[:, 64:].astype(BF16)], axis=1
    )
    grad_normed = scatter_group(split(back_dot(qkv_back, w_qkv).astype(BF16)))
    scale_own = norm_scale(x_own)
    grad_tokens = (
        grad_hidden + norm_back(x_own, scale_own, norm_attn, grad_normed)
    ).astype(BF16)

    result = scatter_group(split(plain_dot(mlp_hidden, w_down_t).astype(BF16)))
    result = (hidden + result).astype(BF16)

    grad_down = trans_dot(mlp_hidden, grad_output)
    grad_gu = trans_dot(mlp_input, grad_both_low)
    sum_ffn_gain = jnp.sum(grad_gu * gate_up.astype(F32), axis=1) / norm_ffn
    grad_gu = grad_gu.astype(BF16)
    piece_gu = sum_z(scatter_fsdp(grad_gu.reshape(8, part_rows, 2 * hid), y, zl))
    piece_down = sum_z(scatter_fsdp(grad_down.astype(BF16).reshape(8, down_rows, width), y, zl))
    piece_down = swap_roles(piece_down)

    grad_out_w = trans_dot(attn_low, hidden_low).astype(BF16)

    def out_block(r, s):
        pair = lax.dynamic_slice_in_dim(grad_out_w, ((x - r) % 4) * 256, 256, 1)
        swap = first if s == 0 else jnp.logical_not(first)
        return jnp.where(swap, pair[:, :128], pair[:, 128:])

    grad_out_t = scatter_group(
        jnp.stack([jnp.stack([out_block(r, s) for s in range(2)]) for r in range(4)])
    )
    grad_out_t = jnp.pad(grad_out_t.reshape(8, part_rows, 128), ((0, 0), (0, 16), (0, 0)))

    grad_qkv_w = trans_dot(normed, qkv_back)
    sum_attn_gain = jnp.sum(grad_qkv_w * w_qkv.astype(F32), axis=1) / norm_attn
    gain_rows = jnp.concatenate(
        [sum_attn_gain.reshape(8, 1, part_rows), sum_ffn_gain.reshape(8, 1, part_rows)], axis=2
    )
    small_rows = jnp.concatenate(
        [
            (gain_sums[0] + gain_sums[1]).reshape(8, 1, 8),
            gain_sums[2].reshape(8, 1, 8),
            jnp.zeros((8, 1, 240), F32),
        ],
        axis=2,
    )
    piece_qkv = jnp.concatenate(
        [
            grad_qkv_w.reshape(8, part_rows, 256),
            gain_rows,
            small_rows,
            jnp.zeros((8, 14, 256), F32),
        ],
        axis=1,
    )
    piece_qkv = jnp.concatenate([piece_qkv, grad_out_t], axis=2).astype(BF16)
    piece_qkv = sum_z(scatter_fsdp(piece_qkv, y, zl))

    def in_order(piece):
        for r, (own, oth) in enumerate(gather_group(piece)):
            yield r, jnp.where(first, own, oth), jnp.where(first, oth, own)

    def columns(pieces, size):
        full = jnp.zeros((part_rows, 8 * size), F32)
        for r, one, two in pieces:
            both = jnp.concatenate([one, two], axis=1).astype(F32)
            full = lax.dynamic_update_slice_in_dim(full, both, ((x - r) % 4) * (2 * size), 1)
        return full

    gu = list(in_order(piece_gu))
    total_gate = columns([(r, a[:, :hid], b[:, :hid]) for r, a, b in gu], hid)
    total_up = columns([(r, a[:, hid:], b[:, hid:]) for r, a, b in gu], hid)
    total_down = jnp.zeros(w_down.shape, F32)
    for r, a, b in in_order(piece_down):
        total_down = lax.dynamic_update_slice_in_dim(
            total_down,
            jnp.concatenate([a, b]).astype(F32),
            ((x - r) % 4) * (2 * down_rows),
            0,
        )
    qkv_pieces = list(in_order(piece_qkv))
    rows_of = slice(0, part_rows)
    total_out = columns([(r, a[rows_of, 256:], b[rows_of, 256:]) for r, a, b in qkv_pieces], 128)
    total_query = columns([(r, a[rows_of, :128], b[rows_of, :128]) for r, a, b in qkv_pieces], 128)
    total_key = columns([(r, a[rows_of, 128:192], b[rows_of, 128:192]) for r, a, b in qkv_pieces], 64)
    total_value = columns([(r, a[rows_of, 192:256], b[rows_of, 192:256]) for r, a, b in qkv_pieces], 64)
    extra = jnp.zeros((8, 2, 256), F32)
    for r, a, b in qkv_pieces:
        both = jnp.stack(
            [a[part_rows : part_rows + 2, :256], b[part_rows : part_rows + 2, :256]]
        ).astype(F32)
        extra = lax.dynamic_update_slice_in_dim(extra, both, ((x - r) % 4) * 2, 0)
    extra = jnp.sum(extra, axis=0)
    return (
        result[None],
        grad_tokens[None],
        extra[0, :part_rows],
        total_query,
        total_key,
        total_value,
        extra[1, :8],
        extra[1, 8:16],
        total_out,
        extra[0, part_rows:],
        total_gate,
        total_up,
        total_down,
    )


def solution(mesh):
    tok, vec, mat = P("fsdp", "ctx", None), P("fsdp"), P("fsdp", None)
    return jax.shard_map(
        local,
        mesh=mesh,
        in_specs=(
            tok, P("fsdp", "ctx"), tok, vec, mat, mat, mat, vec, vec, mat, vec, mat, mat, mat,
        ),
        out_specs=(tok, tok, vec, mat, mat, mat, vec, vec, mat, vec, mat, mat, mat),
        check_vma=False,
    )
```

```python
import functools

import jax
import jax.numpy as jnp
from jax import lax
from jax.experimental import pallas as pl
from jax.experimental.pallas import tpu as pltpu
from jax.sharding import PartitionSpec as P

EPSILON = 1e-05
ROPE_BASE = 1000000.0
F32 = jnp.float32
BF16 = jnp.bfloat16
LOG2E = 1.4426950408889634
SCALE = 0.125


def move_ctx(v, dx=0, dz=0, dc=0):
    pairs = [
        (a * 4 + b * 2 + c, ((a + dx) % 4) * 4 + (b ^ dz) * 2 + (c ^ dc))
        for a in range(4)
        for b in range(2)
        for c in range(2)
    ]
    return lax.ppermute(v, "ctx", pairs)


def move_fsdp(v, dy=0, dz=0):
    pairs = [
        (a * 2 + b, ((a + dy) % 4) * 2 + (b ^ dz)) for a in range(4) for b in range(2)
    ]
    return lax.ppermute(v, "fsdp", pairs)


def swap_roles(v):
    pairs = []
    for t in range(8):
        for h in range(2):
            for f in range(8):
                src = ((t // 2) * 4 + h * 2 + t % 2) * 8 + f
                dst = ((f // 2) * 4 + h * 2 + f % 2) * 8 + t
                pairs.append((src, dst))
    return lax.ppermute(v, ("ctx", "fsdp"), pairs)


def gather_group(u):
    home = move_ctx(u, dc=1)
    away = jnp.stack([move_ctx(u, dx=1), move_ctx(u, dx=2), move_ctx(u, dx=3)])
    other = move_ctx(away, dc=1)
    return [[u, home]] + [[away[r], other[r]] for r in range(3)]


def joined(blocks):
    return jnp.concatenate([b for pair in blocks for b in pair], axis=0)


def scatter_group(part):
    other = move_ctx(part[:, 1].astype(BF16), dc=1)
    total = part[0, 0].astype(F32) + other[0].astype(F32)
    for r in (1, 2, 3):
        acc = part[r, 0].astype(F32) + other[r].astype(F32)
        total = total + move_ctx(acc.astype(BF16), dx=-r).astype(F32)
    return total


def exchange_group(blocks):
    other = move_ctx(jnp.stack([blocks[r][1] for r in range(4)]), dc=1)
    out = [[blocks[0][0], other[0]]]
    for r in (1, 2, 3):
        both = move_ctx(jnp.stack([blocks[r][0], other[r]]), dx=-r)
        out.append([both[0], both[1]])
    return out


def gather_fsdp(u, y, zl):
    o = move_fsdp(u, dz=1)
    low = zl == 0
    pair = jnp.stack([jnp.where(low, u, o), jnp.where(low, o, u)])
    full = jnp.zeros((4,) + pair.shape, u.dtype)
    for d in range(4):
        got = pair if d == 0 else move_fsdp(pair, dy=d)
        full = lax.dynamic_update_index_in_dim(full, got, (y - d) % 4, 0)
    return full.reshape((8,) + u.shape)


def scatter_fsdp(part, y, zl):
    part = part.reshape((4, 2) + part.shape[1:])
    low = zl == 0
    give = jnp.where(low, part[:, 1], part[:, 0]).astype(BF16)
    keep = jnp.where(low, part[:, 0], part[:, 1])
    acc = keep.astype(F32) + move_fsdp(give, dz=1).astype(F32)
    total = lax.dynamic_index_in_dim(acc, y, 0, keepdims=False)
    low = acc.astype(BF16)
    for d in (1, 2, 3):
        give = lax.dynamic_index_in_dim(low, (y + d) % 4, 0, keepdims=False)
        total = total + move_fsdp(give, dy=d).astype(F32)
    return total


def rounded(v):
    return lax.reduce_precision(v, 8, 7)


def sum_z(v):
    mine = rounded(v)
    other = move_ctx(mine.astype(BF16), dz=1)
    return rounded(mine + other.astype(F32)).astype(BF16)


def trans_dot(left, right):
    return lax.dot_general(
        left, right, (((0,), (0,)), ((), ())), preferred_element_type=F32
    )


def back_dot(left, right):
    return lax.dot_general(
        left, right, (((1,), (1,)), ((), ())), preferred_element_type=F32
    )


def plain_dot(left, right):
    return jnp.dot(left, right, preferred_element_type=F32)


def norm_scale(inputs):
    return lax.rsqrt(jnp.mean(inputs * inputs, axis=-1, keepdims=True) + EPSILON)


def norm_back(inputs, scales, gains, grads):
    weighted = grads * gains
    moment = jnp.mean(weighted * inputs, axis=-1, keepdims=True)
    return scales * weighted - inputs * scales * scales * scales * moment


def slot_of(j, x, zh):
    return (x - j // 2) % 4 + 4 * jnp.where(j % 2 == zh, 0, 1)


def attend_kernel(meta, q_ref, k_ref, v_ref, qs_ref, kid_ref, o_ref, ob_ref, l_ref):
    r = pl.program_id(0)
    x, zh = meta[0], meta[1]
    rows = q_ref.shape[2]
    q = q_ref[...].reshape(2 * rows, q_ref.shape[3])
    last = 2 * ((x - r) % 4) + zh
    qid = qs_ref[0, :, 0:1]
    start = qs_ref[0, :, 1:2]

    def step(j, acc):
        slot = slot_of(j, x, zh)
        s = back_dot(q, k_ref[slot])
        kid = kid_ref[slot]
        allowed = (kid <= qid) & (kid >= start)
        w = jnp.exp2(s * (SCALE * LOG2E)).reshape(2, rows, s.shape[1])
        w = jnp.where(allowed[None], w, 0.0).reshape(s.shape)
        return acc + plain_dot(w.astype(BF16), v_ref[slot])

    acc = lax.fori_loop(
        meta[2 + r], last + 1, step, jnp.zeros((2 * rows, v_ref.shape[2]), F32)
    )
    o = acc[:, :64] / acc[:, 64:65]
    o = jnp.concatenate([o[:rows], o[rows:]], axis=1)
    o_ref[0] = o
    ob_ref[0] = o.astype(BF16)
    l_ref[0] = acc.T[64:65]


def attend(meta, q, k, vx, qs, kid):
    rows = q.shape[2]
    full = lambda a: pl.BlockSpec(a.shape, lambda r, m: (0,) * a.ndim)
    return pl.pallas_call(
        attend_kernel,
        grid_spec=pltpu.PrefetchScalarGridSpec(
            num_scalar_prefetch=1,
            grid=(4,),
            in_specs=[
                pl.BlockSpec((2, 1, rows, 64), lambda r, m: (0, r, 0, 0)),
                full(k),
                full(vx),
                pl.BlockSpec((1, rows, 2), lambda r, m: (r, 0, 0)),
                full(kid),
            ],
            out_specs=[
                pl.BlockSpec((1, rows, 128), lambda r, m: (r, 0, 0)),
                pl.BlockSpec((1, rows, 128), lambda r, m: (r, 0, 0)),
                pl.BlockSpec((1, 1, 2 * rows), lambda r, m: (r, 0, 0)),
            ],
        ),
        out_shape=[
            jax.ShapeDtypeStruct((4, rows, 128), F32),
            jax.ShapeDtypeStruct((4, rows, 128), BF16),
            jax.ShapeDtypeStruct((4, 1, 2 * rows), F32),
        ],
        cost_estimate=pl.CostEstimate(
            flops=4_000_000_000, bytes_accessed=6_000_000, transcendentals=6_000_000
        ),
        name="attend",
    )(meta, q, k, vx, qs, kid)


def attend_back_kernel(
    meta, q_ref, do_ref, k_ref, v_ref, lse_ref, delta_ref, qs_ref, kid_ref,
    dq_ref, dk_ref, dv_ref,
):
    r = pl.program_id(0)
    x, zh = meta[0], meta[1]
    rows = q_ref.shape[2]
    q = q_ref[...].reshape(2 * rows, q_ref.shape[3])
    do = do_ref[0]
    do = jnp.concatenate([do[:, :64], do[:, 64:]], axis=0)
    last = 2 * ((x - r) % 4) + zh
    qid = qs_ref[0, 0:1]
    start = qs_ref[0, 1:2]
    lse = lse_ref[0]
    delta = delta_ref[0]

    @pl.when(r == 0)
    def _():
        dk_ref[...] = jnp.zeros_like(dk_ref)
        dv_ref[...] = jnp.zeros_like(dv_ref)

    def step(j, dq):
        slot = slot_of(j, x, zh)
        k = k_ref[slot]
        s = back_dot(k, q)
        kid = kid_ref[slot]
        allowed = (kid <= qid) & (kid >= start)
        p = jnp.where(allowed, jnp.exp2(s * (SCALE * LOG2E) - lse), 0.0)
        dp = back_dot(v_ref[slot], do)
        ds = (p * (dp - delta)).astype(BF16)
        dk_ref[slot] += plain_dot(ds, q)
        dv_ref[slot] += plain_dot(p.astype(BF16), do)
        return dq + trans_dot(ds, k)

    dq = lax.fori_loop(
        meta[2 + r], last + 1, step, jnp.zeros((2 * rows, 64), F32)
    )
    dq_ref[...] = (dq * SCALE).reshape(dq_ref.shape)


def attend_back(meta, q, do, k, v, lse, delta, qs, kid):
    rows = q.shape[2]
    full = lambda a: pl.BlockSpec(a.shape, lambda r, m: (0,) * a.ndim)
    row = lambda n: pl.BlockSpec((1, n, 2 * rows), lambda r, m: (r, 0, 0))
    return pl.pallas_call(
        attend_back_kernel,
        grid_spec=pltpu.PrefetchScalarGridSpec(
            num_scalar_prefetch=1,
            grid=(4,),
            in_specs=[
                pl.BlockSpec((2, 1, rows, 64), lambda r, m: (0, r, 0, 0)),
                pl.BlockSpec((1, rows, 128), lambda r, m: (r, 0, 0)),
                full(k),
                full(v),
                row(1),
                row(1),
                row(2),
                full(kid),
            ],
            out_specs=[
                pl.BlockSpec((2, 1, rows, 64), lambda r, m: (0, r, 0, 0)),
                pl.BlockSpec(k.shape, lambda r, m: (0, 0, 0)),
                pl.BlockSpec(k.shape, lambda r, m: (0, 0, 0)),
            ],
        ),
        out_shape=[
            jax.ShapeDtypeStruct(q.shape, F32),
            jax.ShapeDtypeStruct(k.shape, F32),
            jax.ShapeDtypeStruct(k.shape, F32),
        ],
        cost_estimate=pl.CostEstimate(
            flops=10_000_000_000, bytes_accessed=9_000_000, transcendentals=6_000_000
        ),
        name="attend_back",
    )(meta, q, do, k, v, lse, delta, qs, kid)


def local(
    tokens, positions, cotangent, attn_gain, w_query, w_key, w_value, query_gain,
    key_gain, w_out, ffn_gain, w_gate, w_up, w_down,
):
    ctx, fsdp = lax.axis_index("ctx"), lax.axis_index("fsdp")
    x, zh, c = ctx // 4, (ctx // 2) % 2, ctx % 2
    t = x * 2 + c
    y, zl = fsdp // 2, fsdp % 2
    first = c == 0
    rows = tokens.shape[1]
    width = tokens.shape[2]
    part_rows = w_query.shape[0]
    hidden_all = w_gate.shape[1]
    hid = hidden_all // 8
    toks = 8 * rows

    def half(w, size):
        both = lax.dynamic_slice_in_dim(w, x * (2 * size), 2 * size, 1)
        return jnp.where(first, both[:, :size], both[:, size:])

    pos = positions[0]
    pos_rows = jnp.stack([pos // 64, pos % 64]).astype(F32).astype(BF16)
    pos_rows = jnp.pad(pos_rows, ((0, 14), (0, width - rows)))
    packed = jnp.concatenate([tokens[0], pos_rows], axis=0)
    blocks = gather_group(packed)
    gains = jnp.concatenate([attn_gain, ffn_gain])[None]
    small = jnp.concatenate([query_gain, key_gain, jnp.zeros((240,), BF16)])[None]
    piece = jnp.concatenate(
        [
            jnp.concatenate([half(w_query, 128), half(w_key, 64), half(w_value, 64)], axis=1),
            gains,
            small,
            jnp.zeros((14, 256), BF16),
        ],
        axis=0,
    )
    got = gather_fsdp(piece, y, zl)
    w_qkv = got[:, :part_rows].reshape(width, 256)
    norm_attn = got[:, part_rows, :part_rows].reshape(width).astype(F32)
    norm_ffn = got[:, part_rows, part_rows:].reshape(width).astype(F32)
    norm_query = got[:, part_rows + 1, :8].reshape(64).astype(F32)
    norm_key = got[:, part_rows + 1, 8:16].reshape(64).astype(F32)
    gate_up = jnp.concatenate(
        [half(w_gate, hid), half(w_up, hid), half(w_out, 128)], axis=1
    )
    gate_up = gather_fsdp(gate_up, y, zl).reshape(width, 2 * hid + 128)
    gate_up, out_cols = gate_up[:, : 2 * hid], gate_up[:, 2 * hid :]
    full_out = jnp.zeros((width, width), BF16)
    for r, pair in enumerate(gather_group(out_cols)):
        both = jnp.concatenate(
            [jnp.where(first, pair[0], pair[1]), jnp.where(first, pair[1], pair[0])], axis=1
        )
        full_out = lax.dynamic_update_slice_in_dim(full_out, both, ((x - r) % 4) * 256, 1)
    down_rows = hid // 8
    down = swap_roles(lax.dynamic_slice_in_dim(w_down, t * down_rows, down_rows, 0))
    w_down_t = gather_fsdp(down, y, zl).reshape(hid, width)
    grad_output = joined(gather_group(cotangent[0]))

    x_all = jnp.concatenate([b[:rows] for pair in blocks for b in pair], axis=0)
    pos_hi = jnp.concatenate([b[rows, :rows] for pair in blocks for b in pair])
    pos_lo = jnp.concatenate([b[rows + 1, :rows] for pair in blocks for b in pair])
    token_pos = (pos_hi.astype(F32) * 64.0 + pos_lo.astype(F32)).astype(jnp.int32)
    x_float = x_all.astype(F32)
    normed = (x_float * norm_scale(x_float) * norm_attn).astype(BF16)
    qkv = plain_dot(normed, w_qkv)
    raw = jnp.stack([qkv[:, 0:64], qkv[:, 64:128], qkv[:, 128:192]])
    value_low = qkv[:, 192:].astype(BF16)
    scale_raw = norm_scale(raw)
    gain_raw = jnp.stack([norm_query, norm_query, norm_key])[:, None, :]
    frequency = ROPE_BASE ** (-(jnp.arange(32, dtype=F32) * 2.0 / 64))
    angles = token_pos.astype(F32)[:, None] * frequency[None, :]
    cosines, sines = jnp.cos(angles), jnp.sin(angles)
    cos_all = jnp.concatenate([cosines, cosines], axis=1)
    sin_all = jnp.concatenate([sines, sines], axis=1)
    normal = raw * scale_raw * gain_raw
    turned = jnp.concatenate([-normal[..., 32:], normal[..., :32]], axis=-1)
    rot = (normal * cos_all + turned * sin_all).astype(BF16)
    query_rot = rot[:2].reshape(2, 4, 2 * rows, 64)
    pair_home = jnp.concatenate([rot[2], value_low], axis=1)
    pair_away = move_ctx(pair_home, dz=1)
    pairs = jnp.concatenate([pair_home, pair_away]).reshape(8, 2 * rows, 128)
    keys = pairs[..., :64]
    values = pairs[..., 64:]
    values_one = jnp.concatenate(
        [values, jnp.ones((8, 2 * rows, 1), BF16), jnp.zeros((8, 2 * rows, 63), BF16)], axis=-1
    )
    chips = (x - jnp.arange(4, dtype=jnp.int32)) % 4
    cores = jnp.stack([c, 1 - c]).astype(jnp.int32)
    base = (chips * 4)[:, None] + cores[None, :]
    inner = jnp.arange(rows, dtype=jnp.int32)
    ids = lambda z: ((base + 2 * z)[:, :, None] * rows + inner).reshape(4, 2 * rows)
    query_ids = ids(zh)
    key_ids = jnp.concatenate([query_ids, ids(1 - zh)])
    start_ids = query_ids - token_pos.reshape(4, 2 * rows)
    lowest = jnp.maximum(jnp.min(start_ids, axis=1), 0) // (2 * rows)
    meta = jnp.concatenate([jnp.stack([x, zh]), lowest]).astype(jnp.int32)
    attn_float, attn_part, row_total = attend(
        meta,
        query_rot,
        keys,
        values_one,
        jnp.stack([query_ids, start_ids], axis=-1),
        key_ids[:, None, :],
    )

    part4 = attn_part.reshape(4, 2, rows, 128)
    arrived = exchange_group([[part4[r, 0], part4[r, 1]] for r in range(4)])
    attn_low = jnp.zeros((rows, width), BF16)
    for r in range(4):
        own, oth = arrived[r]
        both = jnp.concatenate([jnp.where(first, own, oth), jnp.where(first, oth, own)], axis=1)
        attn_low = lax.dynamic_update_slice_in_dim(attn_low, both, ((x + r) % 4) * 256, 1)
    x_own = tokens[0].astype(F32)
    hidden = x_own + plain_dot(attn_low, full_out)
    scale_ffn = norm_scale(hidden)
    mlp_own = (hidden * scale_ffn * norm_ffn).astype(BF16)

    mlp_input = joined(gather_group(mlp_own))
    both_proj = plain_dot(mlp_input, gate_up)
    gate_proj, up_proj = both_proj[:, :hid], both_proj[:, hid:]
    grad_mlp = back_dot(grad_output, w_down_t)
    gate_sigmoid = jax.nn.sigmoid(gate_proj)
    mlp_hidden = (gate_proj * gate_sigmoid * up_proj).astype(BF16)
    grad_gate_low = (
        grad_mlp * up_proj * gate_sigmoid * (1.0 + gate_proj * (1.0 - gate_sigmoid))
    ).astype(BF16)
    grad_up_low = (grad_mlp * gate_proj * gate_sigmoid).astype(BF16)
    grad_both_low = jnp.concatenate([grad_gate_low, grad_up_low], axis=1)
    grad_in_part = back_dot(grad_both_low, gate_up)
    split = lambda v: v.reshape((4, 2, rows) + v.shape[1:])
    grad_mlp_input = scatter_group(split(grad_in_part.astype(BF16)))
    grad_hidden = cotangent[0].astype(F32) + norm_back(
        hidden, scale_ffn, norm_ffn, grad_mlp_input
    )
    hidden_low = grad_hidden.astype(BF16)
    grad_attn_own = back_dot(hidden_low, full_out).astype(BF16)

    def head_block(r, s):
        pair = lax.dynamic_slice_in_dim(grad_attn_own, ((x - r) % 4) * 256, 256, 1)
        swap = first if s == 0 else jnp.logical_not(first)
        return jnp.where(swap, pair[:, :128], pair[:, 128:])

    arrived = exchange_group([[head_block(r, s) for s in range(2)] for r in range(4)])
    grad_attn = joined([arrived[(4 - r) % 4] for r in range(4)]).reshape(4, 2 * rows, 128)
    delta = grad_attn.astype(F32) * attn_float
    row_delta = jnp.stack(
        [jnp.sum(delta[..., :64], axis=-1), jnp.sum(delta[..., 64:], axis=-1)], axis=1
    ).reshape(4, 1, 4 * rows)
    twice = lambda v: jnp.concatenate([v, v], axis=-1)
    grad_query, grad_key, grad_value = attend_back(
        meta,
        query_rot,
        grad_attn,
        keys,
        values,
        jnp.log2(row_total),
        row_delta,
        jnp.stack([twice(query_ids), twice(start_ids)], axis=1),
        key_ids[:, :, None],
    )
    pair_grad = jnp.concatenate([grad_key * SCALE, grad_value], axis=-1)
    away = move_ctx(pair_grad[4:].astype(BF16), dz=1)
    pair_grad = (pair_grad[:4] + away.astype(F32)).reshape(toks, 128)
    grad_rot = jnp.concatenate([grad_query.reshape(2, toks, 64), pair_grad[None, :, :64]])
    turned = jnp.concatenate([grad_rot[..., 32:], -grad_rot[..., :32]], axis=-1)
    grad_normal = grad_rot * cos_all + turned * sin_all
    gain_sums = jnp.sum(grad_normal * raw * scale_raw, axis=1)
    raw_back = norm_back(raw, scale_raw, gain_raw, grad_normal).astype(BF16)
    qkv_back = jnp.concatenate(
        [raw_back[0], raw_back[1], raw_back[2], pair_grad[:, 64:].astype(BF16)], axis=1
    )
    grad_normed = scatter_group(split(back_dot(qkv_back, w_qkv).astype(BF16)))
    scale_own = norm_scale(x_own)
    grad_tokens = (
        grad_hidden + norm_back(x_own, scale_own, norm_attn, grad_normed)
    ).astype(BF16)

    result = scatter_group(split(plain_dot(mlp_hidden, w_down_t).astype(BF16)))
    result = (hidden + result).astype(BF16)

    grad_down = trans_dot(mlp_hidden, grad_output)
    grad_gu = trans_dot(mlp_input, grad_both_low)
    sum_ffn_gain = jnp.sum(grad_gu * gate_up.astype(F32), axis=1) / norm_ffn
    grad_gu = grad_gu.astype(BF16)
    piece_gu = sum_z(scatter_fsdp(grad_gu.reshape(8, part_rows, 2 * hid), y, zl))
    piece_down = sum_z(scatter_fsdp(grad_down.astype(BF16).reshape(8, down_rows, width), y, zl))
    piece_down = swap_roles(piece_down)

    grad_out_w = trans_dot(attn_low, hidden_low).astype(BF16)

    def out_block(r, s):
        pair = lax.dynamic_slice_in_dim(grad_out_w, ((x - r) % 4) * 256, 256, 1)
        swap = first if s == 0 else jnp.logical_not(first)
        return jnp.where(swap, pair[:, :128], pair[:, 128:])

    grad_out_t = scatter_group(
        jnp.stack([jnp.stack([out_block(r, s) for s in range(2)]) for r in range(4)])
    )
    grad_out_t = jnp.pad(grad_out_t.reshape(8, part_rows, 128), ((0, 0), (0, 16), (0, 0)))

    grad_qkv_w = trans_dot(normed, qkv_back)
    sum_attn_gain = jnp.sum(grad_qkv_w * w_qkv.astype(F32), axis=1) / norm_attn
    gain_rows = jnp.concatenate(
        [sum_attn_gain.reshape(8, 1, part_rows), sum_ffn_gain.reshape(8, 1, part_rows)], axis=2
    )
    small_rows = jnp.concatenate(
        [
            (gain_sums[0] + gain_sums[1]).reshape(8, 1, 8),
            gain_sums[2].reshape(8, 1, 8),
            jnp.zeros((8, 1, 240), F32),
        ],
        axis=2,
    )
    piece_qkv = jnp.concatenate(
        [
            grad_qkv_w.reshape(8, part_rows, 256),
            gain_rows,
            small_rows,
            jnp.zeros((8, 14, 256), F32),
        ],
        axis=1,
    )
    piece_qkv = jnp.concatenate([piece_qkv, grad_out_t], axis=2).astype(BF16)
    piece_qkv = sum_z(scatter_fsdp(piece_qkv, y, zl))

    def in_order(piece):
        for r, (own, oth) in enumerate(gather_group(piece)):
            yield r, jnp.where(first, own, oth), jnp.where(first, oth, own)

    def columns(pieces, size):
        full = jnp.zeros((part_rows, 8 * size), F32)
        for r, one, two in pieces:
            both = jnp.concatenate([one, two], axis=1).astype(F32)
            full = lax.dynamic_update_slice_in_dim(full, both, ((x - r) % 4) * (2 * size), 1)
        return full

    gu = list(in_order(piece_gu))
    total_gate = columns([(r, a[:, :hid], b[:, :hid]) for r, a, b in gu], hid)
    total_up = columns([(r, a[:, hid:], b[:, hid:]) for r, a, b in gu], hid)
    total_down = jnp.zeros(w_down.shape, F32)
    for r, a, b in in_order(piece_down):
        total_down = lax.dynamic_update_slice_in_dim(
            total_down,
            jnp.concatenate([a, b]).astype(F32),
            ((x - r) % 4) * (2 * down_rows),
            0,
        )
    qkv_pieces = list(in_order(piece_qkv))
    rows_of = slice(0, part_rows)
    total_out = columns([(r, a[rows_of, 256:], b[rows_of, 256:]) for r, a, b in qkv_pieces], 128)
    total_query = columns([(r, a[rows_of, :128], b[rows_of, :128]) for r, a, b in qkv_pieces], 128)
    total_key = columns([(r, a[rows_of, 128:192], b[rows_of, 128:192]) for r, a, b in qkv_pieces], 64)
    total_value = columns([(r, a[rows_of, 192:256], b[rows_of, 192:256]) for r, a, b in qkv_pieces], 64)
    extra = jnp.zeros((8, 2, 256), F32)
    for r, a, b in qkv_pieces:
        both = jnp.stack(
            [a[part_rows : part_rows + 2, :256], b[part_rows : part_rows + 2, :256]]
        ).astype(F32)
        extra = lax.dynamic_update_slice_in_dim(extra, both, ((x - r) % 4) * 2, 0)
    extra = jnp.sum(extra, axis=0)
    return (
        result[None],
        grad_tokens[None],
        extra[0, :part_rows],
        total_query,
        total_key,
        total_value,
        extra[1, :8],
        extra[1, 8:16],
        total_out,
        extra[0, part_rows:],
        total_gate,
        total_up,
        total_down,
    )


def solution(mesh):
    tok, vec, mat = P("fsdp", "ctx", None), P("fsdp"), P("fsdp", None)
    return jax.shard_map(
        local,
        mesh=mesh,
        in_specs=(
            tok, P("fsdp", "ctx"), tok, vec, mat, mat, mat, vec, vec, mat, vec, mat, mat, mat,
        ),
        out_specs=(tok, tok, vec, mat, mat, mat, vec, vec, mat, vec, mat, mat, mat),
        check_vma=False,
    )
```
